32 devices in a mesh: tm: 8 (over y, x, core), panel: 4 (over z).
Axes of the slice: x: 2, y: 2, z: 4, core: 2. Of those that a mesh axis runs over, the one named last changes fastest.
Arguments:
- series: float32 [48, 2048], P(None, 'tm'), may hold values from -20 to 20, as said below
- start_block: float32 [18432, 64], P(('tm', 'panel')), may hold values from -6 to 6
Outputs:
- covariance: float32 [18432, 18432], P(('tm', 'panel'))
- basis: float32 [7, 18432, 64], P(None, ('tm', 'panel'))
- diag_blocks: float32 [6, 64, 64], replicated
- off_blocks: float32 [7, 64, 64], replicated
The draws below stay inside these ranges and needn't reach their ends.
Inputs may be any that keep to these rules, and one draw needn't show every extreme that they name: `series`: each channel has its own scale.
All inputs are finite; a program needn't handle non-finite values.
Results may differ from the reference program's by a relative error of at most 0.0003.
Values sent between devices are 32-bit elements; how exact they have to be, the bound alone decides.
A program may use at most 192 MiB of HBM per device.

```python
import math
import jax
import jax.numpy as jnp
from jax import lax

L = 48
M = 384
B = 64
ITERS = 6
NT = 2048
LM = 18432


def draw_series(key, part):
    scale_key = jax.random.fold_in(key, 11)
    noise_key = jax.random.fold_in(key, 12)
    scales = jnp.exp(jax.random.uniform(scale_key, (L, 1), jnp.float32, math.log(0.3), math.log(3.0)))
    noise = jnp.clip(jax.random.normal(noise_key, (L, NT), jnp.float32), -6.0, 6.0)
    return (scales * noise).astype(jnp.float32)


def block_levels(rng, dims, split, low, top_value):
    def one(axis_at, blocks):
        draws = jax.random.uniform(jax.random.fold_in(jax.random.fold_in(rng, 6), axis_at), (blocks,), jnp.float32, low / len(split), top_value / len(split))
        return jnp.repeat(jnp.exp(draws), dims[axis_at] // blocks).reshape((-1,) + (1,) * (len(dims) - axis_at - 1))

    factor_of = one(*split[0])
    for cut in split[1:]:
        factor_of = factor_of * one(*cut)
    return factor_of


def centred(rng, shape, scale, limit, split=(), kind=jnp.bfloat16):
    array = scale * jax.random.normal(rng, shape, jnp.float32)
    if split:
        array = array * block_levels(rng, shape, split, -0.22, 0.18)
    return jnp.clip(array, -limit, limit).astype(kind)


def setup_inputs(seed: int = 0) -> dict:
    seeds = jax.random.split(jax.random.key(seed), 3)
    return {
        "series": draw_series(jax.random.fold_in(seeds[2], 71), 0),
        "start_block": centred(seeds[1], (LM, B), 1.0, 6.0, ((0, 32),), jnp.float32),
    }


exact_precision = lax.Precision.HIGHEST

def lower_factor(gram_matrix):
    return jnp.linalg.cholesky(gram_matrix)

def reference(series, start_block):
    padded = jnp.concatenate([series, jnp.zeros((L, M), jnp.float32)], axis=1)

    def one_lag(lag_index):
        shifted = lax.dynamic_slice(padded, (jnp.int32(0), lag_index.astype(jnp.int32)), (L, NT))
        return jnp.dot(series.astype(jnp.float32), shifted.T.astype(jnp.float32), precision=exact_precision, preferred_element_type=jnp.float32)
    lag_sums = lax.map(one_lag, jnp.arange(M, dtype=jnp.int32))
    lag_sums = jnp.transpose(lag_sums, (1, 0, 2))
    counts = (NT - jnp.arange(M)).astype(jnp.float32)
    normed = lag_sums / counts[None, :, None]
    two_sided = jnp.concatenate([jnp.transpose(normed, (2, 1, 0))[:, :0:-1, :], normed], axis=1)

    def one_row(lag_index):
        window = lax.dynamic_slice(two_sided, (jnp.int32(0), (M - 1 - lag_index).astype(jnp.int32), jnp.int32(0)), (L, M, L))
        return window.reshape(L, M * L)
    covariance = lax.map(one_row, jnp.arange(M, dtype=jnp.int32)).reshape(M * L, M * L)
    factor = lower_factor(jnp.dot(start_block.T.astype(jnp.float32), start_block.astype(jnp.float32), precision=exact_precision, preferred_element_type=jnp.float32))
    current = jax.scipy.linalg.solve_triangular(factor, start_block.T, lower=True).T
    previous = jnp.zeros_like(current)
    upper = factor.T
    basis_list = [current]
    diagonal_list = []
    upper_list = [upper]
    for iteration in range(ITERS):
        work = jnp.dot(covariance.astype(jnp.float32), current.astype(jnp.float32), precision=exact_precision, preferred_element_type=jnp.float32)
        if iteration > 0:
            work = work - jnp.dot(previous.astype(jnp.float32), upper.T.astype(jnp.float32), precision=exact_precision, preferred_element_type=jnp.float32)
        diagonal = jnp.dot(current.T.astype(jnp.float32), work.astype(jnp.float32), precision=exact_precision, preferred_element_type=jnp.float32)
        work = work - jnp.dot(current.astype(jnp.float32), diagonal.astype(jnp.float32), precision=exact_precision, preferred_element_type=jnp.float32)
        factor = lower_factor(jnp.dot(work.T.astype(jnp.float32), work.astype(jnp.float32), precision=exact_precision, preferred_element_type=jnp.float32))
        upper = factor.T
        previous = current
        current = jax.scipy.linalg.solve_triangular(factor, work.T, lower=True).T
        basis_list.append(current)
        diagonal_list.append(diagonal)
        upper_list.append(upper)
    return (covariance, jnp.stack(basis_list), jnp.stack(diagonal_list), jnp.stack(upper_list))
```

```python
import jax
import jax.numpy as jnp
from jax import lax
from jax.experimental import pallas as pl
from jax.experimental.pallas import tpu as pltpu
from jax.sharding import PartitionSpec as P

M = 384
ITERS = 6


exact_precision = lax.Precision.HIGHEST


def passed_along(block, axis, distance):
    devices = range(lax.axis_size(axis))
    route = [(i - distance, i) for i in devices if i - distance in devices]
    return lax.ppermute(block, axis, route)


def lag_kernel(x_ref, g_ref, o_ref):
    groups, _, width = g_ref.shape
    depth = x_ref.shape[1] // groups
    x = x_ref[...]
    for step in range(o_ref.shape[1] // width):
        window = g_ref[:, step : step + depth, :].reshape(groups * depth, width)
        o_ref[:, step * width : (step + 1) * width] = jnp.dot(
            x, window, precision=exact_precision, preferred_element_type=jnp.float32
        )


def lag_products(local_rows, extended):
    channels, day_count = local_rows.shape
    groups = 8
    width = groups * channels
    depth = day_count // groups
    rows = depth + M // groups
    days = jnp.pad(extended, ((0, 0), (0, max(0, rows * groups + groups - extended.shape[1]))))
    flat = days.T.reshape(-1)
    shifted = jnp.stack(
        [
            lax.slice(flat, (r * channels,), (r * channels + rows * width,)).reshape(rows, width)
            for r in range(groups)
        ]
    )
    by_group = local_rows.reshape(channels, depth, groups).transpose(0, 2, 1)
    return pl.pallas_call(
        lag_kernel,
        out_shape=jax.ShapeDtypeStruct((channels, M * channels), jnp.float32),
        in_specs=[pl.BlockSpec(memory_space=pltpu.VMEM)] * 2,
        out_specs=pl.BlockSpec(memory_space=pltpu.VMEM),
    )(by_group.reshape(channels, day_count), shifted)


def gram_kernel(sizes, q_ref, w_ref, o_ref, held, arrived, send_sem, recv_sem):
    partners = []
    for axis, size in sizes:
        me = lax.axis_index(axis)
        distance = 1
        while distance < size:
            partners.append((axis, me + distance - 2 * distance * ((me // distance) % 2)))
            distance *= 2
    barrier = pltpu.get_barrier_semaphore()
    for axis, other in partners:
        pl.semaphore_signal(
            barrier, inc=1, device_id={axis: other}, device_id_type=pl.DeviceIdType.MESH
        )
    both = jnp.concatenate([q_ref[...], w_ref[...]], axis=1)
    held[0] = lax.dot_general(
        both,
        both,
        (((0,), (0,)), ((), ())),
        precision=exact_precision,
        preferred_element_type=jnp.float32,
    )
    pl.semaphore_wait(barrier, len(partners))
    for step, (axis, other) in enumerate(partners):
        copy = pltpu.make_async_remote_copy(
            src_ref=held.at[step],
            dst_ref=arrived.at[step],
            send_sem=send_sem.at[step],
            recv_sem=recv_sem.at[step],
            device_id={axis: other},
            device_id_type=pl.DeviceIdType.MESH,
        )
        copy.start()
        copy.wait()
        held[step + 1] = held[step] + arrived[step]
    o_ref[...] = held[len(partners)]


def grams(q, w):
    sizes = [("tm", lax.axis_size("tm")), ("panel", lax.axis_size("panel"))]
    steps = sum(size.bit_length() - 1 for _, size in sizes)
    width = q.shape[1] + w.shape[1]
    out = pl.pallas_call(
        lambda *refs: gram_kernel(sizes, *refs),
        out_shape=jax.ShapeDtypeStruct((width, width), jnp.float32),
        in_specs=[pl.BlockSpec(memory_space=pltpu.VMEM)] * 2,
        out_specs=pl.BlockSpec(memory_space=pltpu.VMEM),
        scratch_shapes=[
            pltpu.VMEM((steps + 1, width, width), jnp.float32),
            pltpu.VMEM((steps, width, width), jnp.float32),
            pltpu.SemaphoreType.DMA((steps,)),
            pltpu.SemaphoreType.DMA((steps,)),
        ],
        compiler_params=pltpu.CompilerParams(collective_id=0, has_side_effects=True),
    )(q, w)
    half = q.shape[1]
    return out[:half, :half], out[:half, half:], out[half:, half:]


def local(series, start_block):
    channels, day_count = series.shape
    tm_size = lax.axis_size("tm")
    panel_size = lax.axis_size("panel")
    total_days = day_count * tm_size
    reach_hops = (M - 1 + day_count - 1) // day_count
    pieces = [series]
    moving = series
    for distance in range(reach_hops):
        moving = passed_along(moving, "tm", -1)
        pieces.append(moving)
    extended = jnp.concatenate(pieces, axis=1)
    summed = lax.psum(lag_products(series, extended), "tm")
    counts = (total_days - jnp.arange(M)).astype(jnp.float32)
    counts = (total_days - jnp.arange(M * channels) // channels).astype(jnp.float32)
    normed = summed / counts[None, :]
    blocks = normed.reshape(channels, M, channels)
    before = jnp.transpose(blocks, (2, 1, 0))[:, :0:-1, :].reshape(channels, (M - 1) * channels)
    two_sided = jnp.concatenate([before, normed], axis=1)
    lags_here = M // (tm_size * panel_size)
    block_index = lax.axis_index("tm") * panel_size + lax.axis_index("panel")
    first = (M - lags_here - block_index * lags_here) * channels
    near = lax.dynamic_slice(
        two_sided, (jnp.int32(0), first), (channels, (M + lags_here - 1) * channels)
    )
    row_list = []
    for offset in range(lags_here):
        start = (lags_here - 1 - offset) * channels
        row_list.append(near[:, start : start + M * channels])
    covariance = jnp.concatenate(row_list, axis=0)

    factor = jnp.linalg.cholesky(grams(start_block, start_block)[0])
    current = jax.scipy.linalg.solve_triangular(factor, start_block.T, lower=True).T
    previous = jnp.zeros_like(current)
    upper = factor.T
    basis_list = [current]
    diagonal_list = []
    upper_list = [upper]
    for iteration in range(ITERS):
        work = jnp.dot(
            covariance,
            lax.all_gather(current, ("tm", "panel"), axis=0, tiled=True),
            precision=lax.Precision.HIGH,
            preferred_element_type=jnp.float32,
        )
        if iteration > 0:
            work = work - jnp.dot(
                previous, upper.T, precision=exact_precision, preferred_element_type=jnp.float32
            )
        basis_gram, diagonal, work_gram = grams(current, work)
        work = work - jnp.dot(
            current, diagonal, precision=exact_precision, preferred_element_type=jnp.float32
        )
        cross_term = jnp.dot(
            diagonal.T, diagonal, precision=exact_precision, preferred_element_type=jnp.float32
        )
        weighted = jnp.dot(
            diagonal.T,
            jnp.dot(
                basis_gram, diagonal, precision=exact_precision, preferred_element_type=jnp.float32
            ),
            precision=exact_precision,
            preferred_element_type=jnp.float32,
        )
        gram_matrix = work_gram - 2.0 * cross_term + weighted
        factor = jnp.linalg.cholesky(gram_matrix)
        upper = factor.T
        previous = current
        current = jax.scipy.linalg.solve_triangular(factor, work.T, lower=True).T
        basis_list.append(current)
        diagonal_list.append(diagonal)
        upper_list.append(upper)
    return (covariance, jnp.stack(basis_list), jnp.stack(diagonal_list), jnp.stack(upper_list))


def solution(mesh):
    placed = (P(None, "tm"), P(("tm", "panel"), None))
    return jax.shard_map(
        local,
        mesh=mesh,
        in_specs=placed,
        out_specs=(P(("tm", "panel"), None), P(None, ("tm", "panel"), None), P(), P()),
        check_vma=False,
    )
```
